512 devices in a mesh: layer: 32 (over y_lo, x, core), plane: 16 (over z, y_hi).
Axes of the slice: x: 4, y: 8 (y_hi: 2, y_lo: 4; y = y_hi * 4 + y_lo), z: 8, core: 2. Of those that a mesh axis runs over, the one named last changes fastest.
Arguments:
- sources: bfloat16 [32, 32, 2, 128, 128], P('layer', 'plane'), may hold values from -6 to 6
- operator_tiles: float32 [32, 384, 2, 128, 128], P('layer', 'plane'), may hold values from -0.109375 to 0.109375
- tile_rows: int32 [32, 384], P('layer', 'plane'), may hold values from 0 to 1, as said below
- tile_cols: int32 [32, 384], P('layer', 'plane'), may hold values from 0 to 5, as said below
- send_blocks: int32 [16, 2, 1], P('plane'), may hold values from 0 to 1
Outputs:
- traces: float32 [32, 32, 2, 128, 128], P('layer', 'plane')
The draws below stay inside these ranges and needn't reach their ends.
Inputs may be any that keep to these rules, and one draw needn't show every extreme that they name: Entries of tile_rows lie in 0..1; in each layer and plane piece every row block has exactly 12 tiles, and among them at least one reads each of the four parts of the extended trace (arrived blocks, lower neighbour's, upper neighbour's, own trace). Entries of tile_cols index the extended trace of their piece.
All inputs are finite; a program needn't handle non-finite values.
Results may differ from the reference program's by a relative error of at most 0.0003.
Values sent between devices are 32-bit elements; how exact they have to be, the bound alone decides.
A program may use at most 64 MiB of HBM per device.

```python
import jax
import jax.numpy as jnp
from jax import lax

BS = 128
NB = 2
NK = 1
TILES = 24
SHOTS = 128
TICKS = 3
LAYERS = 32
PIECES = 16
BLOCKS = 32
TILES_ALL = 384


def tile_pattern(key):
    key_order = jax.random.fold_in(key, 71)
    key_chosen = jax.random.fold_in(key, 72)
    count = LAYERS * PIECES
    positions = jnp.arange(TILES, dtype=jnp.int32)
    row_blocks = positions % NB
    category = positions // NB % 4
    chosen = jax.random.randint(key_chosen, (count, TILES), 0, NB * NK, dtype=jnp.int32)
    col_blocks = jnp.where(category[None, :] == 0, chosen % NB, jnp.where(category[None, :] == 1, NB + chosen % NK, jnp.where(category[None, :] == 2, NB + NK + chosen % NK, NB + 2 * NK + chosen % NB)))
    subkeys = jax.random.split(key_order, count)
    shuffle = jax.vmap(lambda one: jax.random.permutation(one, TILES))(subkeys)
    rows_out = jnp.take(row_blocks, shuffle, axis=0)
    cols_out = jnp.take_along_axis(col_blocks, shuffle, axis=1)
    return (rows_out.reshape(LAYERS, PIECES * TILES), cols_out.reshape(LAYERS, PIECES * TILES))


def draw_tile_rows(key, part):
    return tile_pattern(key)[0].astype(jnp.int32)


def draw_tile_cols(key, part):
    return tile_pattern(key)[1].astype(jnp.int32)


def with_ends(array, stream_key, least, top_value):
    place = [jax.random.randint(jax.random.fold_in(stream_key, axis), (), 0, length) for axis, length in enumerate(array.shape)]
    widest = array.shape.index(max(array.shape))
    next_to = place[:widest] + [(place[widest] + 1) % array.shape[widest]] + place[widest + 1:]
    return array.at[tuple(place)].set(least).at[tuple(next_to)].set(top_value)


def steps_of(stream_key, shape, cuts, smallest, high):
    level, own = 1.0, jax.random.fold_in(stream_key, 6)
    for axis_at, parts in cuts:
        steps = jnp.exp(jax.random.uniform(jax.random.fold_in(own, axis_at), (parts,), jnp.float32, smallest / len(cuts), high / len(cuts)))
        level = level * jnp.repeat(steps, shape[axis_at] // parts).reshape([-1 if axis == axis_at else 1 for axis in range(len(shape))])
    return level


def gaussian(key, dims, width, limit, cuts=(), held_as=jnp.bfloat16):
    values = jax.random.normal(key, dims, jnp.float32) * width
    if len(cuts) > 0:
        values = steps_of(key, dims, cuts, -0.22, 0.18) * values
    return jnp.clip(values, min=-limit, max=limit).astype(held_as)


def setup_inputs(seed: int = 0) -> dict:
    keys = jax.random.split(jax.random.key(seed), 6)
    return {
        "sources": gaussian(keys[0], (LAYERS, BLOCKS, 2, BS, SHOTS), 1.0, 6.0, ((0, 32), (1, 16))),
        "operator_tiles": gaussian(keys[1], (LAYERS, TILES_ALL, 2, BS, BS), (2 * BS * TILES // NB) ** -0.5, 0.109375, ((0, 32), (1, 16)), jnp.float32),
        "tile_rows": draw_tile_rows(jax.random.fold_in(keys[5], 71), 0),
        "tile_cols": draw_tile_cols(jax.random.fold_in(keys[5], 71), 0),
        "send_blocks": with_ends(jax.random.randint(keys[4], (PIECES, 2, NK), 0, NB), jax.random.fold_in(keys[4], 1), 0, NB - 1).astype(jnp.int32),
    }


def apply_piece(extended, mats, rows, cols):
    highest = lax.Precision.HIGHEST
    operands = jnp.take(extended, cols, axis=0)
    real_real = jnp.einsum('tij,tjs->tis', mats[:, 0], operands[:, 0], precision=highest)
    imag_imag = jnp.einsum('tij,tjs->tis', mats[:, 1], operands[:, 1], precision=highest)
    real_imag = jnp.einsum('tij,tjs->tis', mats[:, 0], operands[:, 1], precision=highest)
    imag_real = jnp.einsum('tij,tjs->tis', mats[:, 1], operands[:, 0], precision=highest)
    products = jnp.stack([real_real - imag_imag, real_imag + imag_real], axis=1)
    row_select = (rows[None, :] == jnp.arange(NB, dtype=jnp.int32)[:, None]).astype(products.dtype)
    return jnp.einsum('bt,tcis->bcis', row_select, products, precision=highest)


def reference(sources, operator_tiles, tile_rows, tile_cols, send_blocks):
    source_now = sources.astype(jnp.float32).reshape(LAYERS, PIECES, NB, 2, BS, SHOTS)
    mats_all = operator_tiles.reshape(LAYERS, PIECES, TILES, 2, BS, BS)
    rows_all = tile_rows.reshape(LAYERS, PIECES, TILES)
    cols_all = tile_cols.reshape(LAYERS, PIECES, TILES)
    traces = jnp.zeros_like(source_now)
    pieces_index = jnp.arange(PIECES, dtype=jnp.int32)[:, None]
    for repeat in range(TICKS):
        arrived = jnp.concatenate([jnp.zeros_like(traces[:1]), traces[:-1]], axis=0)
        to_lower = arrived[:, pieces_index, send_blocks[:, 0, :]]
        to_upper = arrived[:, pieces_index, send_blocks[:, 1, :]]
        blank = jnp.zeros_like(to_upper[:, :1])
        from_lower = jnp.concatenate([blank, to_upper[:, :-1]], axis=1)
        from_upper = jnp.concatenate([to_lower[:, 1:], blank], axis=1)
        extended = jnp.concatenate([arrived, from_lower, from_upper, traces], axis=2)

        def one_layer(packed):
            return jax.vmap(apply_piece)(*packed)

        fresh = lax.map(one_layer, (extended, mats_all, rows_all, cols_all))
        traces = fresh + source_now
    return traces.reshape(LAYERS, BLOCKS, 2, BS, SHOTS)
```

```python
import jax
import jax.numpy as jnp
from jax import lax
from jax.experimental import pallas as pl
from jax.experimental.pallas import tpu as pltpu
from jax.sharding import PartitionSpec as P

MESH = pl.DeviceIdType.MESH
CHUNKS = 2
PAIRS = 3


def lanes_first(shape, half):
    return lax.broadcasted_iota(jnp.int32, shape, len(shape) - 1) < half


def swap_halves(x):
    return pltpu.roll(x, x.shape[-1] // 2, x.ndim - 1)


def kernel(layers, pieces, src_hbm, ops_hbm, rows_hbm, cols_hbm, send_hbm, out_ref,
           src, ops, rows, cols, send, weights, left, first, second, last, picked, arrived, beside, partial,
           in_sem, ops_sem, send_sem, recv_sem):
    layer = lax.axis_index("layer")
    piece = lax.axis_index("plane")
    width = src.shape[-1]
    half = width // 2
    tiles = ops.shape[0]

    has_above = layer > 0
    has_below = layer < layers - 1
    has_lower = piece > 0
    has_upper = piece < pieces - 1
    gives = (jnp.logical_and(has_below, has_lower), jnp.logical_and(has_below, has_upper), has_below)
    takes = (jnp.logical_and(has_above, has_lower), jnp.logical_and(has_above, has_upper), has_above)
    targets = ((layer + 1, piece - 1), (layer + 1, piece + 1), (layer + 1, piece))
    sources = ((layer - 1, piece - 1), (layer - 1, piece + 1), (layer - 1, piece))

    barrier = pltpu.get_barrier_semaphore()
    for take, source in zip(takes, sources):
        @pl.when(take)
        def _():
            pl.semaphore_signal(barrier, inc=1, device_id=source, device_id_type=MESH)

    loads = [
        pltpu.make_async_copy(src_hbm.at[0], src, in_sem.at[0]),
        pltpu.make_async_copy(send_hbm, send, in_sem.at[1]),
        pltpu.make_async_copy(rows_hbm, rows, in_sem.at[2]),
        pltpu.make_async_copy(cols_hbm, cols, in_sem.at[3]),
        pltpu.make_async_copy(ops_hbm.at[0], ops, ops_sem),
    ]
    for load in loads:
        load.start()

    def copies(tick, chunk):
        whole = (first, second)[tick]
        made = []
        for kind in range(3):
            if kind == 2:
                here, there = whole.at[chunk], arrived.at[tick, chunk]
            else:
                here, there = picked.at[tick, chunk, kind], beside.at[tick, chunk, 1 - kind]
            slot = 2 if kind == 2 else 1 - kind
            made.append(pltpu.make_async_remote_copy(
                src_ref=here, dst_ref=there, send_sem=send_sem.at[tick, chunk, kind],
                recv_sem=recv_sem.at[tick, chunk, slot], device_id=targets[kind], device_id_type=MESH))
        return made

    moves = [[copies(tick, chunk) for chunk in range(CHUNKS)] for tick in range(2)]

    def send_out(tick, chunk):
        for kind in range(3):
            @pl.when(gives[kind])
            def _():
                moves[tick][chunk][kind].start()

    def wait_in(tick, chunk, slot):
        kind = 2 if slot == 2 else 1 - slot
        @pl.when(takes[slot])
        def _():
            moves[tick][chunk][kind].wait_recv()

    for slot in range(2):
        @pl.when(jnp.logical_not(takes[slot]))
        def _():
            for tick in range(2):
                for chunk in range(CHUNKS):
                    beside[tick, chunk, slot] = jnp.zeros((width, width), jnp.float32)

    @pl.when(jnp.logical_not(has_above))
    def _():
        arrived[...] = jnp.zeros(arrived.shape, jnp.float32)

    low = lanes_first((width, width), half)
    loads[0].wait()
    for block in range(2):
        real = src[block, 0].astype(jnp.float32)
        imag = src[block, 1].astype(jnp.float32)
        first[0, block] = jnp.where(low, real, swap_halves(imag))
        first[1, block] = jnp.where(low, swap_halves(real), imag)
    loads[1].wait()

    def pick(tick, chunk):
        whole = (first, second)[tick]
        for kind in range(2):
            picked[tick, chunk, kind] = whole[chunk, send[0, kind]]

    for chunk in range(CHUNKS):
        pick(0, chunk)
    @pl.when(has_below)
    def _():
        pl.semaphore_wait(barrier, 1 + has_lower.astype(jnp.int32) + has_upper.astype(jnp.int32))
    for chunk in range(CHUNKS):
        send_out(0, chunk)

    loads[2].wait()
    loads[3].wait()
    for t in range(tiles):
        slot = rows[0, t] * 6 + cols[0, t]
        for s in range(12):
            weights[s, t] = jnp.where(slot == s, 1.0, 0.0).astype(jnp.float32)
    loads[4].wait()

    def assemble(step, carry):
        start = pl.multiple_of(step * 16, 16)
        pieces_of = [ops[t, pl.ds(start, 16)] for t in range(tiles)]
        for s in range(12):
            total = weights[s, 0] * pieces_of[0]
            for t in range(1, tiles):
                total += weights[s, t] * pieces_of[t]
            high = total.astype(jnp.bfloat16)
            rest = (total - high.astype(jnp.float32)).astype(jnp.bfloat16)
            r, c = s // 6, s % 6
            at = pl.multiple_of(r * 2 * width + start, 16)
            left[c // 2, pl.ds(at, 16), pl.ds((c % 2) * width, width)] = high
            left[c // 2, pl.ds(at, 16), pl.ds((2 + c % 2) * width, width)] = rest
        return carry

    lax.fori_loop(0, 2 * width // 16, assemble, 0)

    def product(pair, right, exact):
        right = right.reshape(2 * width, width)
        high = right.astype(jnp.bfloat16)
        out = jnp.dot(left[pair], jnp.concatenate([high, high], axis=0), preferred_element_type=jnp.float32)
        if not exact:
            rest = (right - high.astype(jnp.float32)).astype(jnp.bfloat16)
            out += jnp.dot(left[pair, :, : 2 * width], rest, preferred_element_type=jnp.float32)
        return out

    sign = jnp.where(low, -1.0, 1.0).astype(jnp.float32)

    def finish(total, block, chunk):
        at = block * 2 * width
        return total[at : at + width] + sign * swap_halves(total[at + width : at + 2 * width]) + first[chunk, block]

    for tick in range(2):
        whole = (first, second)[tick]
        exact = tick == 0
        if tick == 0:
            for chunk in range(CHUNKS):
                partial[chunk] = product(2, whole[chunk], exact)
        for chunk in range(CHUNKS):
            wait_in(tick, chunk, 2)
            partial[chunk] += product(0, arrived[tick, chunk], exact)
            wait_in(tick, chunk, 0)
            wait_in(tick, chunk, 1)
            total = partial[chunk] + product(1, beside[tick, chunk], exact)
            for block in range(2):
                (second, last)[tick][chunk, block] = finish(total, block, chunk)
            if tick == 0:
                pick(1, chunk)
                send_out(1, chunk)
                partial[chunk] = product(2, second[chunk], False)

    for block in range(2):
        out_ref[0, block, 0] = jnp.where(low, last[0, block], swap_halves(last[1, block]))
        out_ref[0, block, 1] = jnp.where(low, swap_halves(last[0, block]), last[1, block])

    for tick in range(2):
        for chunk in range(CHUNKS):
            for kind in range(3):
                @pl.when(gives[kind])
                def _():
                    moves[tick][chunk][kind].wait_send()


def solution(mesh):
    layers, pieces = mesh.shape["layer"], mesh.shape["plane"]

    def per_device(sources, operator_tiles, tile_rows, tile_cols, send_blocks):
        tiles, width = operator_tiles.shape[1], operator_tiles.shape[3]
        flat = operator_tiles.reshape(1, tiles, 2 * width, width)
        hbm = pl.BlockSpec(memory_space=pltpu.MemorySpace.HBM)

        def body(*refs):
            kernel(layers, pieces, *refs)

        f32 = jnp.float32
        return pl.pallas_call(
            body,
            out_shape=jax.ShapeDtypeStruct(sources.shape, f32),
            in_specs=[hbm] * 5,
            out_specs=pl.BlockSpec(memory_space=pltpu.VMEM),
            scratch_shapes=[
                pltpu.VMEM(sources.shape[1:], jnp.bfloat16),
                pltpu.VMEM(flat.shape[1:], f32),
                pltpu.SMEM(tile_rows.shape, jnp.int32),
                pltpu.SMEM(tile_cols.shape, jnp.int32),
                pltpu.SMEM((1, 2), jnp.int32),
                pltpu.SMEM((12, tiles), f32),
                pltpu.VMEM((PAIRS, 4 * width, 4 * width), jnp.bfloat16),
                pltpu.VMEM((CHUNKS, 2, width, width), f32),
                pltpu.VMEM((CHUNKS, 2, width, width), f32),
                pltpu.VMEM((CHUNKS, 2, width, width), f32),
                pltpu.VMEM((2, CHUNKS, 2, width, width), f32),
                pltpu.VMEM((2, CHUNKS, 2, width, width), f32),
                pltpu.VMEM((2, CHUNKS, 2, width, width), f32),
                pltpu.VMEM((CHUNKS, 4 * width, width), f32),
                pltpu.SemaphoreType.DMA((4,)),
                pltpu.SemaphoreType.DMA,
                pltpu.SemaphoreType.DMA((2, CHUNKS, 3)),
                pltpu.SemaphoreType.DMA((2, CHUNKS, 3)),
            ],
            compiler_params=pltpu.CompilerParams(collective_id=0, has_side_effects=True),
        )(sources, flat, tile_rows, tile_cols, send_blocks.reshape(1, 2))

    placed = (
        P("layer", "plane", None, None, None),
        P("layer", "plane", None, None, None),
        P("layer", "plane"),
        P("layer", "plane"),
        P("plane", None, None),
    )
    return jax.shard_map(
        per_device, mesh=mesh, in_specs=placed, out_specs=P("layer", "plane", None, None, None), check_vma=False
    )
```

```python
import jax
import jax.numpy as jnp
from jax import lax
from jax.experimental import pallas as pl
from jax.experimental.pallas import tpu as pltpu
from jax.sharding import PartitionSpec as P

MESH = pl.DeviceIdType.MESH
CHUNKS = 2
PAIRS = 3
RUN = 8
PASSED = {(0, 0, 1), (0, 1, 1), (1, 0, 1)}


def lanes_first(shape, half):
    return lax.broadcasted_iota(jnp.int32, shape, len(shape) - 1) < half


def swap_halves(x):
    return pltpu.roll(x, x.shape[-1] // 2, x.ndim - 1)


def kernel(layers, pieces, src_hbm, ops_hbm, rows_hbm, cols_hbm, send_hbm, out_ref,
           src, ops, rows, cols, send, weights, left, first, second, last, picked, passed, arrived, beside, partial,
           in_sem, ops_sem, send_sem, pass_sem, recv_sem):
    layer = lax.axis_index("layer")
    piece = lax.axis_index("plane")
    width = src.shape[-1]
    half = width // 2
    tiles = ops.shape[0]

    has_above = layer > 0
    has_below = layer < layers - 1
    has_lower = piece > 0
    has_upper = piece < pieces - 1
    turns = jnp.logical_and((layer + 1) % RUN == 0, has_below)
    relays = jnp.logical_and(layer % RUN == 0, has_above)
    exists = (has_lower, has_upper)
    targets = ((layer + 1, piece - 1), (layer + 1, piece + 1), (layer + 1, piece))

    def both(*conditions):
        out = conditions[0]
        for condition in conditions[1:]:
            out = jnp.logical_and(out, condition)
        return out

    def gives(tick, chunk, kind):
        if kind == 2:
            return has_below
        out = both(has_below, exists[kind])
        return both(out, jnp.logical_not(turns)) if (tick, chunk, kind) in PASSED else out

    takes = (both(has_above, has_lower), both(has_above, has_upper), has_above)
    sources = ((layer - 1, piece - 1), (layer - 1, piece + 1), (layer - 1, piece))

    barrier = pltpu.get_barrier_semaphore()
    for take, source in zip(takes, sources):
        @pl.when(take)
        def _():
            pl.semaphore_signal(barrier, inc=1, device_id=source, device_id_type=MESH)

    @pl.when(both(relays, has_lower))
    def _():
        pl.semaphore_signal(barrier, inc=1, device_id=(layer, piece - 1), device_id_type=MESH)

    loads = [
        pltpu.make_async_copy(src_hbm.at[0], src, in_sem.at[0]),
        pltpu.make_async_copy(send_hbm, send, in_sem.at[1]),
        pltpu.make_async_copy(rows_hbm, rows, in_sem.at[2]),
        pltpu.make_async_copy(cols_hbm, cols, in_sem.at[3]),
        pltpu.make_async_copy(ops_hbm.at[0], ops, ops_sem),
    ]
    for load in loads:
        load.start()

    def copies(tick, chunk):
        whole = (first, second)[tick]
        made = []
        for kind in range(3):
            if kind == 2:
                here, there = whole.at[chunk], arrived.at[tick, chunk]
            else:
                here, there = picked.at[tick, chunk, kind], beside.at[tick, chunk, 1 - kind]
            slot = 2 if kind == 2 else 1 - kind
            made.append(pltpu.make_async_remote_copy(
                src_ref=here, dst_ref=there, send_sem=send_sem.at[tick, chunk, kind],
                recv_sem=recv_sem.at[tick, chunk, slot], device_id=targets[kind], device_id_type=MESH))
        return made

    moves = [[copies(tick, chunk) for chunk in range(CHUNKS)] for tick in range(2)]
    relayed = {
        (tick, chunk, kind): pltpu.make_async_remote_copy(
            src_ref=passed.at[tick, chunk], dst_ref=beside.at[tick, chunk, 1 - kind], send_sem=pass_sem.at[tick, chunk],
            recv_sem=recv_sem.at[tick, chunk, 1 - kind], device_id=(layer, piece + 2 * kind - 1), device_id_type=MESH)
        for tick, chunk, kind in sorted(PASSED)
    }

    def send_out(tick, chunk):
        @pl.when(turns)
        def _():
            moves[tick][chunk][2].start()
        for kind in range(2):
            @pl.when(gives(tick, chunk, kind))
            def _():
                moves[tick][chunk][kind].start()
        @pl.when(both(has_below, jnp.logical_not(turns)))
        def _():
            moves[tick][chunk][2].start()

    def wait_in(tick, chunk, slot, only=None):
        kind = 2 if slot == 2 else 1 - slot
        @pl.when(takes[slot] if only is None else both(takes[slot], only))
        def _():
            moves[tick][chunk][kind].wait_recv()

    def pass_on(tick, chunk):
        for kind in range(2):
            if (tick, chunk, kind) in PASSED:
                @pl.when(both(relays, exists[kind]))
                def _():
                    passed[tick, chunk] = jnp.where(send[0, kind] == 0, arrived[tick, chunk, 0], arrived[tick, chunk, 1])
                    relayed[tick, chunk, kind].start()

    for slot in range(2):
        @pl.when(jnp.logical_not(takes[slot]))
        def _():
            for tick in range(2):
                for chunk in range(CHUNKS):
                    beside[tick, chunk, slot] = jnp.zeros((width, width), jnp.float32)

    @pl.when(jnp.logical_not(has_above))
    def _():
        arrived[...] = jnp.zeros(arrived.shape, jnp.float32)

    low = lanes_first((width, width), half)
    loads[0].wait()
    for block in range(2):
        real = src[block, 0].astype(jnp.float32)
        imag = src[block, 1].astype(jnp.float32)
        first[0, block] = jnp.where(low, real, swap_halves(imag))
        first[1, block] = jnp.where(low, swap_halves(real), imag)
    loads[1].wait()

    def pick(tick, chunk):
        whole = (first, second)[tick]
        for kind in range(2):
            picked[tick, chunk, kind] = whole[chunk, send[0, kind]]

    for chunk in range(CHUNKS):
        pick(0, chunk)
    @pl.when(has_below)
    def _():
        pl.semaphore_wait(barrier, 1 + has_lower.astype(jnp.int32) + has_upper.astype(jnp.int32) * (1 + relays.astype(jnp.int32)))
    for chunk in range(CHUNKS):
        send_out(0, chunk)

    wait_in(0, 0, 2, relays)
    pass_on(0, 0)

    loads[2].wait()
    loads[3].wait()
    for t in range(tiles):
        slot = rows[0, t] * 6 + cols[0, t]
        for s in range(12):
            weights[s, t] = jnp.where(slot == s, 1.0, 0.0).astype(jnp.float32)
    loads[4].wait()

    def assemble(step, carry):
        start = pl.multiple_of(step * 16, 16)
        pieces_of = [ops[t, pl.ds(start, 16)] for t in range(tiles)]
        for s in range(12):
            total = weights[s, 0] * pieces_of[0]
            for t in range(1, tiles):
                total += weights[s, t] * pieces_of[t]
            high = total.astype(jnp.bfloat16)
            rest = (total - high.astype(jnp.float32)).astype(jnp.bfloat16)
            r, c = s // 6, s % 6
            at = pl.multiple_of(r * 2 * width + start, 16)
            left[c // 2, pl.ds(at, 16), pl.ds((c % 2) * width, width)] = high
            left[c // 2, pl.ds(at, 16), pl.ds((2 + c % 2) * width, width)] = rest
        return carry

    lax.fori_loop(0, 2 * width // 16, assemble, 0)

    def product(pair, right, exact):
        right = right.reshape(2 * width, width)
        high = right.astype(jnp.bfloat16)
        out = jnp.dot(left[pair], jnp.concatenate([high, high], axis=0), preferred_element_type=jnp.float32)
        if not exact:
            rest = (right - high.astype(jnp.float32)).astype(jnp.bfloat16)
            out += jnp.dot(left[pair, :, : 2 * width], rest, preferred_element_type=jnp.float32)
        return out

    sign = jnp.where(low, -1.0, 1.0).astype(jnp.float32)

    def finish(total, block, chunk):
        at = block * 2 * width
        return total[at : at + width] + sign * swap_halves(total[at + width : at + 2 * width]) + first[chunk, block]

    wait_in(0, 1, 2, relays)
    pass_on(0, 1)

    for tick in range(2):
        whole = (first, second)[tick]
        exact = tick == 0
        if tick == 0:
            for chunk in range(CHUNKS):
                partial[chunk] = product(2, whole[chunk], exact)
        for chunk in range(CHUNKS):
            if tick == 0:
                wait_in(tick, chunk, 2, jnp.logical_not(relays))
            else:
                wait_in(tick, chunk, 2)
                pass_on(tick, chunk)
            partial[chunk] += product(0, arrived[tick, chunk], exact)
            wait_in(tick, chunk, 0)
            wait_in(tick, chunk, 1)
            total = partial[chunk] + product(1, beside[tick, chunk], exact)
            for block in range(2):
                (second, last)[tick][chunk, block] = finish(total, block, chunk)
            if tick == 0:
                pick(1, chunk)
                send_out(1, chunk)
                partial[chunk] = product(2, second[chunk], False)

    for block in range(2):
        out_ref[0, block, 0] = jnp.where(low, last[0, block], swap_halves(last[1, block]))
        out_ref[0, block, 1] = jnp.where(low, swap_halves(last[0, block]), last[1, block])

    for tick in range(2):
        for chunk in range(CHUNKS):
            for kind in range(3):
                @pl.when(gives(tick, chunk, kind))
                def _():
                    moves[tick][chunk][kind].wait_send()
    for tick, chunk, kind in sorted(PASSED):
        @pl.when(both(relays, exists[kind]))
        def _():
            relayed[tick, chunk, kind].wait_send()


def solution(mesh):
    layers, pieces = mesh.shape["layer"], mesh.shape["plane"]

    def per_device(sources, operator_tiles, tile_rows, tile_cols, send_blocks):
        tiles, width = operator_tiles.shape[1], operator_tiles.shape[3]
        flat = operator_tiles.reshape(1, tiles, 2 * width, width)
        hbm = pl.BlockSpec(memory_space=pltpu.MemorySpace.HBM)

        def body(*refs):
            kernel(layers, pieces, *refs)

        f32 = jnp.float32
        return pl.pallas_call(
            body,
            out_shape=pltpu.VMEM(sources.shape, f32),
            in_specs=[hbm] * 5,
            out_specs=pl.BlockSpec(memory_space=pltpu.VMEM),
            scratch_shapes=[
                pltpu.VMEM(sources.shape[1:], jnp.bfloat16),
                pltpu.VMEM(flat.shape[1:], f32),
                pltpu.SMEM(tile_rows.shape, jnp.int32),
                pltpu.SMEM(tile_cols.shape, jnp.int32),
                pltpu.SMEM((1, 2), jnp.int32),
                pltpu.SMEM((12, tiles), f32),
                pltpu.VMEM((PAIRS, 4 * width, 4 * width), jnp.bfloat16),
                pltpu.VMEM((CHUNKS, 2, width, width), f32),
                pltpu.VMEM((CHUNKS, 2, width, width), f32),
                pltpu.VMEM((CHUNKS, 2, width, width), f32),
                pltpu.VMEM((2, CHUNKS, 2, width, width), f32),
                pltpu.VMEM((2, CHUNKS, width, width), f32),
                pltpu.VMEM((2, CHUNKS, 2, width, width), f32),
                pltpu.VMEM((2, CHUNKS, 2, width, width), f32),
                pltpu.VMEM((CHUNKS, 4 * width, width), f32),
                pltpu.SemaphoreType.DMA((4,)),
                pltpu.SemaphoreType.DMA,
                pltpu.SemaphoreType.DMA((2, CHUNKS, 3)),
                pltpu.SemaphoreType.DMA((2, CHUNKS)),
                pltpu.SemaphoreType.DMA((2, CHUNKS, 3)),
            ],
            compiler_params=pltpu.CompilerParams(collective_id=0, has_side_effects=True),
        )(sources, flat, tile_rows, tile_cols, send_blocks.reshape(1, 2))

    placed = (
        P("layer", "plane", None, None, None),
        P("layer", "plane", None, None, None),
        P("layer", "plane"),
        P("layer", "plane"),
        P("plane", None, None),
    )
    return jax.shard_map(
        per_device, mesh=mesh, in_specs=placed, out_specs=P("layer", "plane", None, None, None), check_vma=False
    )
```

```python
import jax
import jax.numpy as jnp
from jax import lax
from jax.experimental import pallas as pl
from jax.experimental.pallas import tpu as pltpu
from jax.sharding import PartitionSpec as P

MESH = pl.DeviceIdType.MESH
CHUNKS = 2
PAIRS = 3
RUN = 8
LONG = {(0, 0): (7, 15, 23), (0, 1): (7, 15, 23), (1, 0): (23,)}


def lanes_first(shape, half):
    return lax.broadcasted_iota(jnp.int32, shape, len(shape) - 1) < half


def swap_halves(x):
    return pltpu.roll(x, x.shape[-1] // 2, x.ndim - 1)


def kernel(layers, pieces, src_hbm, ops_hbm, rows_hbm, cols_hbm, send_hbm, out_ref,
           src, ops, rows, cols, send, weights, left, first, second, last, picked, passed, arrived, beside, partial,
           in_sem, ops_sem, send_sem, pass_sem, long_sem, recv_sem):
    layer = lax.axis_index("layer")
    piece = lax.axis_index("plane")
    width = src.shape[-1]
    half = width // 2
    tiles = ops.shape[0]

    has_above = layer > 0
    has_below = layer < layers - 1
    has_lower = piece > 0
    has_upper = piece < pieces - 1
    turns = jnp.logical_and((layer + 1) % RUN == 0, has_below)
    lands = jnp.logical_and(layer % RUN == 0, has_above)
    stands = jnp.logical_and((layer + 1) % RUN == 0, layer != 2 * RUN - 1)

    def long_way(of_layer, of_piece, back):
        crossing = of_layer == (RUN - 1 if back else 3 * RUN - 1)
        other = of_piece + 1 - 2 * (of_piece % 2)
        there = jnp.where(crossing, (3 * RUN if back else RUN) - 1, of_layer + (-2 if back else 2) * RUN)
        return there, jnp.where(crossing, other, of_piece)

    helper = long_way(layer, piece, False)
    helped = long_way(layer, piece, True)
    helps = jnp.logical_and(stands, helped[1] < pieces - 1)
    landing = long_way(layer - 1, piece - 1, False)
    exists = (has_lower, has_upper)
    targets = ((layer + 1, piece - 1), (layer + 1, piece + 1), (layer + 1, piece))

    def both(*conditions):
        out = conditions[0]
        for condition in conditions[1:]:
            out = jnp.logical_and(out, condition)
        return out

    def among(which, layers_named):
        out = which == layers_named[0]
        for named in layers_named[1:]:
            out = jnp.logical_or(out, which == named)
        return out

    def goes_long(tick, chunk):
        return among(layer, LONG[tick, chunk])

    def helps_long(tick, chunk):
        return both(helps, among(helped[0], LONG[tick, chunk]))

    def gives(tick, chunk, kind):
        if kind == 2:
            return has_below
        out = both(has_below, exists[kind])
        return both(out, jnp.logical_not(goes_long(tick, chunk))) if kind == 1 and (tick, chunk) in LONG else out

    takes = (both(has_above, has_lower), both(has_above, has_upper), has_above)
    sources = ((layer - 1, piece - 1), (layer - 1, piece + 1), (layer - 1, piece))

    barrier = pltpu.get_barrier_semaphore()
    for take, source in zip(takes, sources):
        @pl.when(take)
        def _():
            pl.semaphore_signal(barrier, inc=1, device_id=source, device_id_type=MESH)

    @pl.when(both(lands, has_lower))
    def _():
        pl.semaphore_signal(barrier, inc=1, device_id=landing, device_id_type=MESH)

    @pl.when(helps)
    def _():
        pl.semaphore_signal(barrier, inc=1, device_id=helped, device_id_type=MESH)

    loads = [
        pltpu.make_async_copy(src_hbm.at[0], src, in_sem.at[0]),
        pltpu.make_async_copy(send_hbm, send, in_sem.at[1]),
        pltpu.make_async_copy(rows_hbm, rows, in_sem.at[2]),
        pltpu.make_async_copy(cols_hbm, cols, in_sem.at[3]),
        pltpu.make_async_copy(ops_hbm.at[0], ops, ops_sem),
    ]
    for load in loads:
        load.start()

    def copies(tick, chunk):
        whole = (first, second)[tick]
        made = []
        for kind in range(3):
            if kind == 2:
                here, there = whole.at[chunk], arrived.at[tick, chunk]
            else:
                here, there = picked.at[tick, chunk, kind], beside.at[tick, chunk, 1 - kind]
            slot = 2 if kind == 2 else 1 - kind
            made.append(pltpu.make_async_remote_copy(
                src_ref=here, dst_ref=there, send_sem=send_sem.at[tick, chunk, kind],
                recv_sem=recv_sem.at[tick, chunk, slot], device_id=targets[kind], device_id_type=MESH))
        return made

    moves = [[copies(tick, chunk) for chunk in range(CHUNKS)] for tick in range(2)]
    sent_long, passed_on = {}, {}
    for at, (tick, chunk) in enumerate(LONG):
        sent_long[tick, chunk] = pltpu.make_async_remote_copy(
            src_ref=picked.at[tick, chunk, 1], dst_ref=passed.at[at], send_sem=send_sem.at[tick, chunk, 1],
            recv_sem=long_sem.at[at], device_id=helper, device_id_type=MESH)
        passed_on[tick, chunk] = pltpu.make_async_remote_copy(
            src_ref=passed.at[at], dst_ref=beside.at[tick, chunk, 0], send_sem=pass_sem.at[at],
            recv_sem=recv_sem.at[tick, chunk, 0], device_id=(helped[0] + 1, helped[1] + 1), device_id_type=MESH)

    def send_out(tick, chunk):
        if (tick, chunk) in LONG:
            @pl.when(both(goes_long(tick, chunk), has_upper))
            def _():
                sent_long[tick, chunk].start()
        for kind in range(3):
            @pl.when(gives(tick, chunk, kind))
            def _():
                moves[tick][chunk][kind].start()

    def wait_in(tick, chunk, slot):
        kind = 2 if slot == 2 else 1 - slot
        @pl.when(takes[slot])
        def _():
            moves[tick][chunk][kind].wait_recv()

    def pass_on(tick, chunk):
        if (tick, chunk) in LONG:
            @pl.when(helps_long(tick, chunk))
            def _():
                sent_long[tick, chunk].wait_recv()
                passed_on[tick, chunk].start()

    for slot in range(2):
        @pl.when(jnp.logical_not(takes[slot]))
        def _():
            for tick in range(2):
                for chunk in range(CHUNKS):
                    beside[tick, chunk, slot] = jnp.zeros((width, width), jnp.float32)

    @pl.when(jnp.logical_not(has_above))
    def _():
        arrived[...] = jnp.zeros(arrived.shape, jnp.float32)

    low = lanes_first((width, width), half)
    loads[0].wait()
    for block in range(2):
        real = src[block, 0].astype(jnp.float32)
        imag = src[block, 1].astype(jnp.float32)
        first[0, block] = jnp.where(low, real, swap_halves(imag))
        first[1, block] = jnp.where(low, swap_halves(real), imag)
    loads[1].wait()

    def pick(tick, chunk):
        whole = (first, second)[tick]
        for kind in range(2):
            picked[tick, chunk, kind] = whole[chunk, send[0, kind]]

    for chunk in range(CHUNKS):
        pick(0, chunk)
    def count(condition):
        return condition.astype(jnp.int32)

    below = count(has_below) * (1 + count(has_lower) + count(has_upper)) + count(both(turns, has_upper)) + count(helps)

    @pl.when(below > 0)
    def _():
        pl.semaphore_wait(barrier, below)
    for chunk in range(CHUNKS):
        send_out(0, chunk)

    pass_on(0, 0)

    loads[2].wait()
    loads[3].wait()
    for t in range(tiles):
        slot = rows[0, t] * 6 + cols[0, t]
        for s in range(12):
            weights[s, t] = jnp.where(slot == s, 1.0, 0.0).astype(jnp.float32)
    loads[4].wait()

    def assemble(step, carry):
        start = pl.multiple_of(step * 16, 16)
        pieces_of = [ops[t, pl.ds(start, 16)] for t in range(tiles)]
        for s in range(12):
            total = weights[s, 0] * pieces_of[0]
            for t in range(1, tiles):
                total += weights[s, t] * pieces_of[t]
            high = total.astype(jnp.bfloat16)
            rest = (total - high.astype(jnp.float32)).astype(jnp.bfloat16)
            r, c = s // 6, s % 6
            at = pl.multiple_of(r * 2 * width + start, 16)
            left[c // 2, pl.ds(at, 16), pl.ds((c % 2) * width, width)] = high
            left[c // 2, pl.ds(at, 16), pl.ds((2 + c % 2) * width, width)] = rest
        return carry

    lax.fori_loop(0, 2 * width // 16, assemble, 0)

    def product(pair, right, exact):
        right = right.reshape(2 * width, width)
        high = right.astype(jnp.bfloat16)
        out = jnp.dot(left[pair], jnp.concatenate([high, high], axis=0), preferred_element_type=jnp.float32)
        if not exact:
            rest = (right - high.astype(jnp.float32)).astype(jnp.bfloat16)
            out += jnp.dot(left[pair, :, : 2 * width], rest, preferred_element_type=jnp.float32)
        return out

    sign = jnp.where(low, -1.0, 1.0).astype(jnp.float32)

    def finish(total, block, chunk):
        at = block * 2 * width
        return total[at : at + width] + sign * swap_halves(total[at + width : at + 2 * width]) + first[chunk, block]

    pass_on(0, 1)

    for tick in range(2):
        if tick == 1:
            pass_on(1, 0)
            pass_on(1, 1)
        whole = (first, second)[tick]
        exact = tick == 0
        if tick == 0:
            for chunk in range(CHUNKS):
                partial[chunk] = product(2, whole[chunk], exact)
        for chunk in range(CHUNKS):
            wait_in(tick, chunk, 2)
            partial[chunk] += product(0, arrived[tick, chunk], exact)
            wait_in(tick, chunk, 0)
            wait_in(tick, chunk, 1)
            total = partial[chunk] + product(1, beside[tick, chunk], exact)
            for block in range(2):
                (second, last)[tick][chunk, block] = finish(total, block, chunk)
            if tick == 0:
                pick(1, chunk)
                send_out(1, chunk)
                partial[chunk] = product(2, second[chunk], False)

    for block in range(2):
        out_ref[0, block, 0] = jnp.where(low, last[0, block], swap_halves(last[1, block]))
        out_ref[0, block, 1] = jnp.where(low, swap_halves(last[0, block]), last[1, block])

    for tick in range(2):
        for chunk in range(CHUNKS):
            for kind in range(3):
                @pl.when(gives(tick, chunk, kind))
                def _():
                    moves[tick][chunk][kind].wait_send()
    for tick, chunk in LONG:
        @pl.when(both(goes_long(tick, chunk), has_upper))
        def _():
            sent_long[tick, chunk].wait_send()
        @pl.when(helps_long(tick, chunk))
        def _():
            passed_on[tick, chunk].wait_send()


def solution(mesh):
    layers, pieces = mesh.shape["layer"], mesh.shape["plane"]

    def per_device(sources, operator_tiles, tile_rows, tile_cols, send_blocks):
        tiles, width = operator_tiles.shape[1], operator_tiles.shape[3]
        flat = operator_tiles.reshape(1, tiles, 2 * width, width)
        hbm = pl.BlockSpec(memory_space=pltpu.MemorySpace.HBM)

        def body(*refs):
            kernel(layers, pieces, *refs)

        f32 = jnp.float32
        return pl.pallas_call(
            body,
            out_shape=pltpu.VMEM(sources.shape, f32),
            in_specs=[hbm] * 5,
            out_specs=pl.BlockSpec(memory_space=pltpu.VMEM),
            scratch_shapes=[
                pltpu.VMEM(sources.shape[1:], jnp.bfloat16),
                pltpu.VMEM(flat.shape[1:], f32),
                pltpu.SMEM(tile_rows.shape, jnp.int32),
                pltpu.SMEM(tile_cols.shape, jnp.int32),
                pltpu.SMEM((1, 2), jnp.int32),
                pltpu.SMEM((12, tiles), f32),
                pltpu.VMEM((PAIRS, 4 * width, 4 * width), jnp.bfloat16),
                pltpu.VMEM((CHUNKS, 2, width, width), f32),
                pltpu.VMEM((CHUNKS, 2, width, width), f32),
                pltpu.VMEM((CHUNKS, 2, width, width), f32),
                pltpu.VMEM((2, CHUNKS, 2, width, width), f32),
                pltpu.VMEM((len(LONG), width, width), f32),
                pltpu.VMEM((2, CHUNKS, 2, width, width), f32),
                pltpu.VMEM((2, CHUNKS, 2, width, width), f32),
                pltpu.VMEM((CHUNKS, 4 * width, width), f32),
                pltpu.SemaphoreType.DMA((4,)),
                pltpu.SemaphoreType.DMA,
                pltpu.SemaphoreType.DMA((2, CHUNKS, 3)),
                pltpu.SemaphoreType.DMA((len(LONG),)),
                pltpu.SemaphoreType.DMA((len(LONG),)),
                pltpu.SemaphoreType.DMA((2, CHUNKS, 3)),
            ],
            compiler_params=pltpu.CompilerParams(collective_id=0, has_side_effects=True),
        )(sources, flat, tile_rows, tile_cols, send_blocks.reshape(1, 2))

    placed = (
        P("layer", "plane", None, None, None),
        P("layer", "plane", None, None, None),
        P("layer", "plane"),
        P("layer", "plane"),
        P("plane", None, None),
    )
    return jax.shard_map(
        per_device, mesh=mesh, in_specs=placed, out_specs=P("layer", "plane", None, None, None), check_vma=False
    )
```

```python
import jax
import jax.numpy as jnp
from jax import lax
from jax.experimental import pallas as pl
from jax.experimental.pallas import tpu as pltpu
from jax.sharding import PartitionSpec as P

MESH = pl.DeviceIdType.MESH
CHUNKS = 2
PAIRS = 3
RUN = 8
LONG = {(0, 0): (7, 15, 23), (0, 1): (7, 15, 23), (1, 0): (23,)}


def lanes_first(shape, half):
    return lax.broadcasted_iota(jnp.int32, shape, len(shape) - 1) < half


def swap_halves(x):
    return pltpu.roll(x, x.shape[-1] // 2, x.ndim - 1)


def kernel(layers, pieces, src_hbm, ops_hbm, rows_hbm, cols_hbm, send_hbm, out_ref,
           src, ops, rows, cols, send, weights, left, first, second, last, picked, passed, arrived, beside, partial,
           in_sem, ops_sem, send_sem, pass_sem, long_sem, recv_sem):
    layer = lax.axis_index("layer")
    piece = lax.axis_index("plane")
    width = src.shape[-1]
    half = width // 2
    tiles = ops.shape[0]

    has_above = layer > 0
    has_below = layer < layers - 1
    has_lower = piece > 0
    has_upper = piece < pieces - 1
    turns = jnp.logical_and((layer + 1) % RUN == 0, has_below)
    lands = jnp.logical_and(layer % RUN == 0, has_above)
    stands = jnp.logical_and((layer + 1) % RUN == 0, layer != 2 * RUN - 1)

    def long_way(of_layer, of_piece, back):
        crossing = of_layer == (RUN - 1 if back else 3 * RUN - 1)
        other = of_piece + 1 - 2 * (of_piece % 2)
        there = jnp.where(crossing, (3 * RUN if back else RUN) - 1, of_layer + (-2 if back else 2) * RUN)
        return there, jnp.where(crossing, other, of_piece)

    helper = long_way(layer, piece, False)
    helped = long_way(layer, piece, True)
    helps = jnp.logical_and(stands, helped[1] < pieces - 1)
    landing = long_way(layer - 1, piece - 1, False)
    exists = (has_lower, has_upper)
    targets = ((layer + 1, piece - 1), (layer + 1, piece + 1), (layer + 1, piece))

    def both(*conditions):
        out = conditions[0]
        for condition in conditions[1:]:
            out = jnp.logical_and(out, condition)
        return out

    def among(which, layers_named):
        out = which == layers_named[0]
        for named in layers_named[1:]:
            out = jnp.logical_or(out, which == named)
        return out

    def goes_long(tick, chunk):
        return among(layer, LONG[tick, chunk])

    def helps_long(tick, chunk):
        return both(helps, among(helped[0], LONG[tick, chunk]))

    def gives(tick, chunk, kind):
        if kind == 2:
            return has_below
        out = both(has_below, exists[kind])
        return both(out, jnp.logical_not(goes_long(tick, chunk))) if kind == 1 and (tick, chunk) in LONG else out

    takes = (both(has_above, has_lower), both(has_above, has_upper), has_above)
    sources = ((layer - 1, piece - 1), (layer - 1, piece + 1), (layer - 1, piece))

    barrier = pltpu.get_barrier_semaphore()
    for take, source in zip(takes, sources):
        @pl.when(take)
        def _():
            pl.semaphore_signal(barrier, inc=1, device_id=source, device_id_type=MESH)

    @pl.when(both(lands, has_lower))
    def _():
        pl.semaphore_signal(barrier, inc=1, device_id=landing, device_id_type=MESH)

    @pl.when(helps)
    def _():
        pl.semaphore_signal(barrier, inc=1, device_id=helped, device_id_type=MESH)

    loads = [
        pltpu.make_async_copy(src_hbm.at[0], src, in_sem.at[0]),
        pltpu.make_async_copy(send_hbm, send, in_sem.at[1]),
        pltpu.make_async_copy(rows_hbm, rows, in_sem.at[2]),
        pltpu.make_async_copy(cols_hbm, cols, in_sem.at[3]),
        pltpu.make_async_copy(ops_hbm.at[0], ops, ops_sem),
    ]
    for load in loads:
        load.start()

    def copies(tick, chunk):
        whole = (first, second)[tick]
        made = []
        for kind in range(3):
            if kind == 2:
                here, there = whole.at[chunk], arrived.at[tick, chunk]
            else:
                here, there = picked.at[tick, chunk, kind], beside.at[tick, chunk, 1 - kind]
            slot = 2 if kind == 2 else 1 - kind
            made.append(pltpu.make_async_remote_copy(
                src_ref=here, dst_ref=there, send_sem=send_sem.at[tick, chunk, kind],
                recv_sem=recv_sem.at[tick, chunk, slot], device_id=targets[kind], device_id_type=MESH))
        return made

    moves = [[copies(tick, chunk) for chunk in range(CHUNKS)] for tick in range(2)]
    sent_long, passed_on = {}, {}
    for at, (tick, chunk) in enumerate(LONG):
        sent_long[tick, chunk] = pltpu.make_async_remote_copy(
            src_ref=picked.at[tick, chunk, 1], dst_ref=passed.at[at], send_sem=send_sem.at[tick, chunk, 1],
            recv_sem=long_sem.at[at], device_id=helper, device_id_type=MESH)
        passed_on[tick, chunk] = pltpu.make_async_remote_copy(
            src_ref=passed.at[at], dst_ref=beside.at[tick, chunk, 0], send_sem=pass_sem.at[at],
            recv_sem=recv_sem.at[tick, chunk, 0], device_id=(helped[0] + 1, helped[1] + 1), device_id_type=MESH)

    def send_out(tick, chunk):
        if (tick, chunk) in LONG:
            @pl.when(both(goes_long(tick, chunk), has_upper))
            def _():
                sent_long[tick, chunk].start()
        for kind in (2, 0, 1):
            @pl.when(gives(tick, chunk, kind))
            def _():
                moves[tick][chunk][kind].start()

    def wait_in(tick, chunk, slot):
        kind = 2 if slot == 2 else 1 - slot
        @pl.when(takes[slot])
        def _():
            moves[tick][chunk][kind].wait_recv()

    def pass_on(tick, chunk):
        if (tick, chunk) in LONG:
            @pl.when(helps_long(tick, chunk))
            def _():
                sent_long[tick, chunk].wait_recv()
                passed_on[tick, chunk].start()

    for slot in range(2):
        @pl.when(jnp.logical_not(takes[slot]))
        def _():
            for tick in range(2):
                for chunk in range(CHUNKS):
                    beside[tick, chunk, slot] = jnp.zeros((width, width), jnp.float32)

    @pl.when(jnp.logical_not(has_above))
    def _():
        arrived[...] = jnp.zeros(arrived.shape, jnp.float32)

    low = lanes_first((width, width), half)
    loads[0].wait()
    for block in range(2):
        real = src[block, 0].astype(jnp.float32)
        imag = src[block, 1].astype(jnp.float32)
        first[0, block] = jnp.where(low, real, swap_halves(imag))
        first[1, block] = jnp.where(low, swap_halves(real), imag)
    loads[1].wait()

    def pick(tick, chunk):
        whole = (first, second)[tick]
        for kind in range(2):
            picked[tick, chunk, kind] = whole[chunk, send[0, kind]]

    for chunk in range(CHUNKS):
        pick(0, chunk)
    def count(condition):
        return condition.astype(jnp.int32)

    below = count(has_below) * (1 + count(has_lower) + count(has_upper)) + count(both(turns, has_upper)) + count(helps)

    @pl.when(below > 0)
    def _():
        pl.semaphore_wait(barrier, below)
    for chunk in range(CHUNKS):
        send_out(0, chunk)

    pass_on(0, 0)

    loads[2].wait()
    loads[3].wait()
    for t in range(tiles):
        slot = rows[0, t] * 6 + cols[0, t]
        for s in range(12):
            weights[s, t] = jnp.where(slot == s, 1.0, 0.0).astype(jnp.float32)
    loads[4].wait()

    def assemble(step, carry):
        start = pl.multiple_of(step * 16, 16)
        pieces_of = [ops[t, pl.ds(start, 16)] for t in range(tiles)]
        for s in range(12):
            total = weights[s, 0] * pieces_of[0]
            for t in range(1, tiles):
                total += weights[s, t] * pieces_of[t]
            high = total.astype(jnp.bfloat16)
            rest = (total - high.astype(jnp.float32)).astype(jnp.bfloat16)
            r, c = s // 6, s % 6
            at = pl.multiple_of(r * 2 * width + start, 16)
            left[c // 2, pl.ds(at, 16), pl.ds((c % 2) * width, width)] = high
            left[c // 2, pl.ds(at, 16), pl.ds((2 + c % 2) * width, width)] = rest
        return carry

    lax.fori_loop(0, 2 * width // 16, assemble, 0)

    def product(pair, right, exact):
        right = right.reshape(2 * width, width)
        high = right.astype(jnp.bfloat16)
        out = jnp.dot(left[pair], jnp.concatenate([high, high], axis=0), preferred_element_type=jnp.float32)
        if not exact:
            rest = (right - high.astype(jnp.float32)).astype(jnp.bfloat16)
            out += jnp.dot(left[pair, :, : 2 * width], rest, preferred_element_type=jnp.float32)
        return out

    sign = jnp.where(low, -1.0, 1.0).astype(jnp.float32)

    def finish(total, block, chunk):
        at = block * 2 * width
        return total[at : at + width] + sign * swap_halves(total[at + width : at + 2 * width]) + first[chunk, block]

    pass_on(0, 1)

    for tick in range(2):
        if tick == 1:
            pass_on(1, 0)
            pass_on(1, 1)
        whole = (first, second)[tick]
        exact = tick == 0
        if tick == 0:
            for chunk in range(CHUNKS):
                partial[chunk] = product(2, whole[chunk], exact)
        for chunk in range(CHUNKS):
            wait_in(tick, chunk, 2)
            partial[chunk] += product(0, arrived[tick, chunk], exact)
            wait_in(tick, chunk, 0)
            wait_in(tick, chunk, 1)
            total = partial[chunk] + product(1, beside[tick, chunk], exact)
            for block in range(2):
                (second, last)[tick][chunk, block] = finish(total, block, chunk)
            if tick == 0:
                pick(1, chunk)
                send_out(1, chunk)
                partial[chunk] = product(2, second[chunk], False)

    for block in range(2):
        out_ref[0, block, 0] = jnp.where(low, last[0, block], swap_halves(last[1, block]))
        out_ref[0, block, 1] = jnp.where(low, swap_halves(last[0, block]), last[1, block])

    for tick in range(2):
        for chunk in range(CHUNKS):
            for kind in range(3):
                @pl.when(gives(tick, chunk, kind))
                def _():
                    moves[tick][chunk][kind].wait_send()
    for tick, chunk in LONG:
        @pl.when(both(goes_long(tick, chunk), has_upper))
        def _():
            sent_long[tick, chunk].wait_send()
        @pl.when(helps_long(tick, chunk))
        def _():
            passed_on[tick, chunk].wait_send()


def solution(mesh):
    layers, pieces = mesh.shape["layer"], mesh.shape["plane"]

    def per_device(sources, operator_tiles, tile_rows, tile_cols, send_blocks):
        tiles, width = operator_tiles.shape[1], operator_tiles.shape[3]
        flat = operator_tiles.reshape(1, tiles, 2 * width, width)
        hbm = pl.BlockSpec(memory_space=pltpu.MemorySpace.HBM)

        def body(*refs):
            kernel(layers, pieces, *refs)

        f32 = jnp.float32
        return pl.pallas_call(
            body,
            out_shape=pltpu.VMEM(sources.shape, f32),
            in_specs=[hbm] * 5,
            out_specs=pl.BlockSpec(memory_space=pltpu.VMEM),
            scratch_shapes=[
                pltpu.VMEM(sources.shape[1:], jnp.bfloat16),
                pltpu.VMEM(flat.shape[1:], f32),
                pltpu.SMEM(tile_rows.shape, jnp.int32),
                pltpu.SMEM(tile_cols.shape, jnp.int32),
                pltpu.SMEM((1, 2), jnp.int32),
                pltpu.SMEM((12, tiles), f32),
                pltpu.VMEM((PAIRS, 4 * width, 4 * width), jnp.bfloat16),
                pltpu.VMEM((CHUNKS, 2, width, width), f32),
                pltpu.VMEM((CHUNKS, 2, width, width), f32),
                pltpu.VMEM((CHUNKS, 2, width, width), f32),
                pltpu.VMEM((2, CHUNKS, 2, width, width), f32),
                pltpu.VMEM((len(LONG), width, width), f32),
                pltpu.VMEM((2, CHUNKS, 2, width, width), f32),
                pltpu.VMEM((2, CHUNKS, 2, width, width), f32),
                pltpu.VMEM((CHUNKS, 4 * width, width), f32),
                pltpu.SemaphoreType.DMA((4,)),
                pltpu.SemaphoreType.DMA,
                pltpu.SemaphoreType.DMA((2, CHUNKS, 3)),
                pltpu.SemaphoreType.DMA((len(LONG),)),
                pltpu.SemaphoreType.DMA((len(LONG),)),
                pltpu.SemaphoreType.DMA((2, CHUNKS, 3)),
            ],
            compiler_params=pltpu.CompilerParams(collective_id=0, has_side_effects=True),
        )(sources, flat, tile_rows, tile_cols, send_blocks.reshape(1, 2))

    placed = (
        P("layer", "plane", None, None, None),
        P("layer", "plane", None, None, None),
        P("layer", "plane"),
        P("layer", "plane"),
        P("plane", None, None),
    )
    return jax.shard_map(
        per_device, mesh=mesh, in_specs=placed, out_specs=P("layer", "plane", None, None, None), check_vma=False
    )
```
